32 devices in a mesh: item: 8 (over y, x, core), dp: 4 (over z).
Axes of the slice: x: 2, y: 2, z: 4, core: 2. Of those that a mesh axis runs over, the one named last changes fastest.
Arguments:
- hidden_states: bfloat16 [32768, 512], P(('item', 'dp'))
- item_table: bfloat16 [4096, 512], P('item'), may hold values from -0.25 to 0.25
- cand_local: int32 [64], replicated, may hold values from 0 to 511
- log_sample: float32 [64], replicated, may hold values from -14 to -4
- target_slot: int32 [32768], P(('item', 'dp')), may hold values from 0 to 63
- loss_weight: float32 [32768], P(('item', 'dp')), may hold values from -6 to 6
Outputs:
- grad_hidden: bfloat16 [32768, 512], P(('item', 'dp'))
- grad_table: float32 [4096, 512], P('item')
The draws below stay inside these ranges and needn't reach their ends.
Inputs may be any that keep to these rules, and one draw needn't show every extreme that they name: Candidate slot s belongs to the item shard s // 8; cand_local counts rows within that shard, and a row may be sampled more than once.
All inputs are finite; a program needn't handle non-finite values.
Results may differ from the reference program's by a relative error of at most 0.0049.
Values may be sent and summed in bfloat16 or wider, within the bound.
No kernel may reach another device: no remote copies, remote signals or barrier semaphores. Data moves between devices by JAX's collectives and lax.ppermute only.
A program may use at most 64 MiB of HBM per device.

```python
import math
import jax
import jax.numpy as jnp
import numpy as np
from jax import lax

D = 512
CAND_DEV = 8
ROWS_DEV = 512
NC = 64
ITEMS = 4096
TOKENS = 32768


def draw_hidden_states(key, part):
    first = jax.random.fold_in(key, 0)
    values = jax.random.normal(first, (TOKENS, D), jnp.float32)
    return values.astype(jnp.bfloat16)


def touch_ends(entries, own_key, low, largest):
    shape = entries.shape
    place = [jax.random.randint(jax.random.fold_in(own_key, axis), (), 0, shape[axis]) for axis in range(len(shape))]
    entries = entries.at[tuple(place)].set(low)
    longest = shape.index(max(shape))
    place[longest] = (place[longest] + 1) % shape[longest]
    return entries.at[tuple(place)].set(largest)


def block_levels(key, dims, cuts, least, high):
    loudness = 1.0
    for axis_at, shards_of in cuts:
        draws = jax.random.uniform(jax.random.fold_in(jax.random.fold_in(key, 6), axis_at), (shards_of,), jnp.float32, least / len(cuts), high / len(cuts))
        loudness = loudness * jnp.repeat(jnp.exp(draws), dims[axis_at] // shards_of).reshape((-1,) + (1,) * (len(dims) - 1 - axis_at))
    return loudness


def rank_table(number_of, lean):
    loads = [(1 << 20) // math.isqrt(grade ** lean) + 1 for grade in range(1, number_of + 1)]
    scale = 1 + sum(loads) // (1 << 30)
    return np.cumsum(np.array([max(1, weight // scale) for weight in loads]))


def ranked(own_key, shape, number_of, lean):
    table = rank_table(number_of, lean)
    lot = jax.random.randint(jax.random.fold_in(own_key, 1), shape, 0, int(table[number_of - 1]))
    grade = jnp.searchsorted(jnp.asarray(table, jnp.int32), lot, side="right")
    return jax.random.permutation(jax.random.fold_in(own_key, 2), number_of)[grade].astype(jnp.int32)


def normal_values(own_key, dims, scale, most, cuts=(), kind=jnp.bfloat16):
    result = jax.random.normal(own_key, dims, jnp.float32) * scale
    if len(cuts) > 0:
        result = block_levels(own_key, dims, cuts, -0.22, 0.18) * result
    return jnp.clip(result, min=-most, max=most).astype(kind)


def setup_inputs(seed: int = 0) -> dict:
    key_of = jax.random.split(jax.random.key(seed), 7)
    return {
        "hidden_states": draw_hidden_states(jax.random.fold_in(key_of[6], 71), 0),
        "item_table": normal_values(key_of[1], (ITEMS, D), D ** -0.5, 0.25, ((0, 8),)),
        "cand_local": touch_ends(ranked(key_of[2], (NC,), ROWS_DEV, 2), jax.random.fold_in(key_of[2], 3), 0, ROWS_DEV - 1).astype(jnp.int32),
        "log_sample": jnp.clip(jax.random.uniform(key_of[3], (NC,), jnp.float32, -14.0, -4.0), -14.0, -4.0),
        "target_slot": touch_ends(jax.random.randint(key_of[4], (TOKENS,), 0, NC), jax.random.fold_in(key_of[4], 1), 0, NC - 1).astype(jnp.int32),
        "loss_weight": normal_values(key_of[5], (TOKENS,), 1.0, 6.0, ((0, 32),), jnp.float32),
    }


def reference(hidden_states, item_table, cand_local, log_sample, target_slot, loss_weight):
    slots = jnp.arange(NC, dtype=jnp.int32)
    item_ids = ((slots // CAND_DEV) * ROWS_DEV + cand_local).astype(jnp.int32)
    cand_rows = item_table[item_ids]
    block = math.gcd(TOKENS, 4096)
    count = TOKENS // block
    states = hidden_states.reshape(count, block, D)
    targets = target_slot.reshape(count, block)
    weights = loss_weight.reshape(count, block)

    def step(total, inputs):
        rows, tgt, wts = inputs
        logits = jnp.dot(rows, cand_rows.T, preferred_element_type=jnp.float32) - log_sample[None, :]
        probs = jax.nn.softmax(logits, axis=1)
        onehot = (tgt[:, None] == slots[None, :]).astype(jnp.float32)
        grad_logits = (wts[:, None] * (probs - onehot)).astype(jnp.bfloat16)
        grad_rows = jnp.dot(grad_logits, cand_rows, preferred_element_type=jnp.float32).astype(jnp.bfloat16)
        total = total + jnp.dot(grad_logits.T, rows, preferred_element_type=jnp.float32)
        return total, grad_rows

    grad_cand, grad_hidden = lax.scan(step, jnp.zeros((NC, D), jnp.float32), (states, targets, weights))
    grad_table = jnp.zeros((ITEMS, D), jnp.float32).at[item_ids].add(grad_cand)
    return grad_hidden.reshape(TOKENS, D), grad_table
```

```python
import jax
import jax.numpy as jnp
from jax import lax
from jax.sharding import PartitionSpec as P

AXES = ("item", "dp")


def exchange(value, axis, mask):
    size = lax.axis_size(axis)
    return lax.ppermute(value, axis, [(i, i ^ mask) for i in range(size)])


def levels_of(size):
    levels, bit = [], 2
    while bit < size:
        if 2 * bit < size:
            levels.append((bit ^ 1, (2 * bit) ^ 1, (3 * bit) ^ 1))
            bit *= 4
        else:
            levels.append((bit ^ 1,))
            bit *= 2
    return levels


def gather_rows(mine):
    size = lax.axis_size("item")
    blocks = {0: mine}
    if size > 1:
        blocks[1] = exchange(mine, "item", 1)
    for masks in levels_of(size):
        held = sorted(blocks)
        fresh = {}
        for mask in masks[::-1]:
            order = sorted(held, key=lambda k: k ^ mask)
            got = exchange(jnp.concatenate([blocks[k] for k in order]), "item", mask)
            for place, piece in zip(order, jnp.split(got, len(order))):
                fresh[place ^ mask] = piece
        blocks.update(fresh)
    return jnp.concatenate([blocks[k] for k in range(size)])


def scatter_sum(blocks):
    size = lax.axis_size("item")
    levels = ([(1,)] if size > 1 else []) + levels_of(size)
    kept = [{0}]
    for masks in levels[::-1]:
        kept.append({mask ^ k for mask in (0,) + masks for k in kept[-1]})
    kept = kept[::-1]
    assert len(kept[0]) == size
    for masks, rest in zip(levels, kept[1:]):
        order = sorted(rest)
        got = []
        for mask in masks[::-1]:
            out = jnp.concatenate([blocks[k ^ mask] for k in order]).astype(jnp.bfloat16)
            got.append(exchange(out, "item", mask))
        sums = {}
        for place, k in enumerate(order):
            total = blocks[k]
            for piece in got:
                step = piece.shape[0] // len(order)
                total = total + piece[place * step : (place + 1) * step].astype(jnp.float32)
            sums[k] = total
        blocks = sums
    return blocks[0]


def batch_sum(value):
    size = lax.axis_size("dp")
    bit = 1
    while bit < size:
        mine = value.astype(jnp.bfloat16)
        if 2 * bit < size:
            far = exchange(mine, "dp", 3 * bit)
            mid = exchange(mine, "dp", 2 * bit)
            near = exchange(mine, "dp", bit)
            wide = [v.astype(jnp.float32) for v in (mine, near, mid, far)]
            value = (wide[0] + wide[1]) + (wide[2] + wide[3])
            bit *= 4
        else:
            other = exchange(mine, "dp", bit)
            value = mine.astype(jnp.float32) + other.astype(jnp.float32)
            bit *= 2
    return value


def on_device(hidden_states, item_table, cand_local, log_sample, target_slot, loss_weight):
    owners = lax.axis_size("item")
    total_cands = log_sample.shape[0]
    per_owner = total_cands // owners
    my_index = lax.axis_index("item")
    my_local = lax.dynamic_slice_in_dim(cand_local, my_index * per_owner, per_owner)
    table_rows = item_table.shape[0]
    my_rows = item_table[my_local]
    cand_rows = gather_rows(my_rows)
    place = jnp.arange(total_cands, dtype=jnp.int32)
    slots = ((place // per_owner) ^ my_index) * per_owner + place % per_owner
    log_q = log_sample[slots]
    logits = jnp.dot(cand_rows, hidden_states.T, preferred_element_type=jnp.float32) - log_q[:, None]
    probs = jax.nn.softmax(logits, axis=0)
    onehot = (target_slot[None, :] == slots[:, None]).astype(jnp.float32)
    grad_logits = (loss_weight[None, :] * (probs - onehot)).astype(jnp.bfloat16)
    partial = jnp.dot(grad_logits, hidden_states, preferred_element_type=jnp.float32)
    grad_hidden = jnp.dot(grad_logits.T, cand_rows, preferred_element_type=jnp.float32).astype(
        jnp.bfloat16
    )
    terms = {k: partial[k * per_owner : (k + 1) * per_owner] for k in range(owners)}
    owned = batch_sum(scatter_sum(terms))
    placing = (my_local[:, None] == jnp.arange(table_rows, dtype=jnp.int32)[None, :]).astype(
        jnp.float32
    )
    grad_table = jnp.dot(
        placing.T, owned, preferred_element_type=jnp.float32, precision=lax.Precision.HIGHEST
    )
    return (grad_hidden, grad_table)


def solution(mesh):
    placed = (
        P(AXES, None),
        P("item", None),
        P(),
        P(),
        P(AXES),
        P(AXES),
    )
    return jax.shard_map(
        on_device,
        mesh=mesh,
        in_specs=placed,
        out_specs=(P(AXES, None), P("item", None)),
        check_vma=False,
    )
```

```python
import jax
import jax.numpy as jnp
from jax import lax
from jax.sharding import PartitionSpec as P

AXES = ("item", "dp")


def exchange(value, axis, mask):
    size = lax.axis_size(axis)
    return lax.ppermute(value, axis, [(i, i ^ mask) for i in range(size)])


def levels_of(size):
    levels, bit = [], 2
    while bit < size:
        if 2 * bit < size:
            levels.append((bit ^ 1, (2 * bit) ^ 1, (3 * bit) ^ 1))
            bit *= 4
        else:
            levels.append((bit ^ 1,))
            bit *= 2
    return levels


def gather_rows(mine):
    size = lax.axis_size("item")
    blocks = {0: mine}
    if size > 1:
        blocks[1] = exchange(mine, "item", 1)
    for masks in levels_of(size):
        held = sorted(blocks)
        fresh = {}
        for mask in masks:
            order = sorted(held, key=lambda k: k ^ mask)
            got = exchange(jnp.concatenate([blocks[k] for k in order]), "item", mask)
            for place, piece in zip(order, jnp.split(got, len(order))):
                fresh[place ^ mask] = piece
        blocks.update(fresh)
    return jnp.concatenate([blocks[k] for k in range(size)])


def scatter_sum(blocks):
    size = lax.axis_size("item")
    levels = ([(1,)] if size > 1 else []) + levels_of(size)
    kept = [{0}]
    for masks in levels[::-1]:
        kept.append({mask ^ k for mask in (0,) + masks for k in kept[-1]})
    kept = kept[::-1]
    assert len(kept[0]) == size
    for masks, rest in zip(levels, kept[1:]):
        order = sorted(rest)
        got = []
        for mask in masks:
            out = jnp.concatenate([blocks[k ^ mask] for k in order]).astype(jnp.bfloat16)
            got.append(exchange(out, "item", mask))
        sums = {}
        for place, k in enumerate(order):
            total = blocks[k]
            for piece in got:
                step = piece.shape[0] // len(order)
                total = total + piece[place * step : (place + 1) * step].astype(jnp.float32)
            sums[k] = total
        blocks = sums
    return blocks[0]


def batch_sum(value):
    size = lax.axis_size("dp")
    bit = 1
    while bit < size:
        mine = value.astype(jnp.bfloat16)
        if 2 * bit < size:
            near = exchange(mine, "dp", bit)
            mid = exchange(mine, "dp", 2 * bit)
            far = exchange(mine, "dp", 3 * bit)
            wide = [v.astype(jnp.float32) for v in (mine, near, mid, far)]
            value = (wide[0] + wide[1]) + (wide[2] + wide[3])
            bit *= 4
        else:
            other = exchange(mine, "dp", bit)
            value = mine.astype(jnp.float32) + other.astype(jnp.float32)
            bit *= 2
    return value


def three_pieces(value):
    pieces = []
    for _ in range(3):
        piece = lax.reduce_precision(value, 8, 7)
        pieces.append(piece.astype(jnp.bfloat16))
        value = value - piece
    return pieces


def on_device(hidden_states, item_table, cand_local, log_sample, target_slot, loss_weight):
    owners = lax.axis_size("item")
    total_cands = log_sample.shape[0]
    per_owner = total_cands // owners
    my_index = lax.axis_index("item")
    my_local = lax.dynamic_slice_in_dim(cand_local, my_index * per_owner, per_owner)
    table_rows = item_table.shape[0]
    rows = jnp.arange(table_rows, dtype=jnp.int32)
    placing = (my_local[:, None] == rows[None, :]).astype(jnp.bfloat16)
    my_rows = jnp.dot(placing, item_table, preferred_element_type=jnp.float32).astype(jnp.bfloat16)
    cand_rows = gather_rows(my_rows)
    place = jnp.arange(total_cands, dtype=jnp.int32)
    slots = ((place // per_owner) ^ my_index) * per_owner + place % per_owner
    log_q = jnp.sum(jnp.where(slots[:, None] == place[None, :], log_sample[None, :], 0.0), axis=1)
    logits = jnp.dot(cand_rows, hidden_states.T, preferred_element_type=jnp.float32) - log_q[:, None]
    probs = jax.nn.softmax(logits, axis=0)
    onehot = (target_slot[None, :] == slots[:, None]).astype(jnp.float32)
    grad_logits = (loss_weight[None, :] * (probs - onehot)).astype(jnp.bfloat16)
    partial = jnp.dot(grad_logits, hidden_states, preferred_element_type=jnp.float32)
    grad_hidden = jnp.dot(grad_logits.T, cand_rows, preferred_element_type=jnp.float32).astype(
        jnp.bfloat16
    )
    terms = {k: partial[k * per_owner : (k + 1) * per_owner] for k in range(owners)}
    owned = batch_sum(scatter_sum(terms))
    grad_table = jnp.dot(
        jnp.concatenate([placing] * 3).T,
        jnp.concatenate(three_pieces(owned)),
        preferred_element_type=jnp.float32,
    )
    return (grad_hidden, grad_table)


def solution(mesh):
    placed = (
        P(AXES, None),
        P("item", None),
        P(),
        P(),
        P(AXES),
        P(AXES),
    )
    return jax.shard_map(
        on_device,
        mesh=mesh,
        in_specs=placed,
        out_specs=(P(AXES, None), P("item", None)),
        check_vma=False,
    )
```
